32 devices in a mesh: field: 4 (over y, x), gz: 8 (over z, core).
Axes of the slice: x: 2, y: 2, z: 4, core: 2. Of those that a mesh axis runs over, the one named last changes fastest.
Arguments:
- fields: bfloat16 [2048, 2, 8, 16, 256], P('gz', None, 'field'), may hold values from -8 to 8
- shells: int32 [2048, 16, 256], P('gz'), may hold values from 0 to 255
- mubins: int32 [2048, 16, 256], P('gz'), may hold values from 0 to 7, as said below
Outputs:
- power: float32 [3, 8, 256], replicated
The draws below stay inside these ranges and needn't reach their ends.
Inputs may be any that keep to these rules, and one draw needn't show every extreme that they name: `mubins`: A cell's mu-bin index is never above its k-shell index.
All inputs are finite; a program needn't handle non-finite values.
Results may differ from the reference program's by a relative error of at most 0.00052.
Values may be sent and summed in bfloat16 or wider, within the bound.
A program may use at most 192 MiB of HBM per device.

```python
import math
import jax
import jax.numpy as jnp
import numpy as np
from jax import lax

NZ = 2048
FIELDS = 8
SHELLS = 256
MUBINS = 8
PLANES = 16
YROWS = 256
N_FIELD = 4


def draw_fields(key, part):
    first_key, second_key, third_key = jax.random.split(jax.random.fold_in(key, 11), 3)
    common = jax.random.normal(first_key, (NZ, 2, 1, PLANES, YROWS), jnp.float32)
    mixing = jax.random.uniform(second_key, (FIELDS,), jnp.float32, 0.5, 1.0).at[0].set(1.0)
    noise = jax.random.normal(third_key, (NZ, 2, FIELDS, PLANES, YROWS), jnp.float32)
    values = mixing[None, None, :, None, None] * common + 0.7 * noise
    return jnp.clip(values, -8.0, 8.0).astype(jnp.bfloat16)


def shell_and_mu(key):
    shell_key, mu_key = jax.random.split(jax.random.fold_in(key, 23))
    shell_ids = jax.random.randint(shell_key, (NZ, PLANES, YROWS), 0, SHELLS, jnp.int32)
    upper = jnp.minimum(shell_ids + 1, MUBINS)
    mu_ids = jax.random.randint(mu_key, (NZ, PLANES, YROWS), 0, upper, jnp.int32)
    return (shell_ids, mu_ids)


def draw_shells(key, part):
    return shell_and_mu(key)[0]


def draw_mubins(key, part):
    return shell_and_mu(key)[1]


def setup_inputs(seed: int = 0) -> dict:
    seeds = jax.random.split(jax.random.key(seed), 4)
    return {
        "fields": draw_fields(jax.random.fold_in(seeds[3], 71), 0),
        "shells": draw_shells(jax.random.fold_in(seeds[3], 71), 0),
        "mubins": draw_mubins(jax.random.fold_in(seeds[3], 71), 0),
    }


def make_coef():
    table = np.zeros((3, 8, 7), np.float32)
    table[0, 0, 0] = 1.0
    table[1, 1, 0] = 1.0
    table[2, 1, 0] = -0.5
    table[2, 2, 1] = 1.5
    table[2, 3, 2] = 1.5
    table[2, 4, 3] = 1.5
    table[2, 5, 4] = 3.0
    table[2, 6, 5] = 3.0
    table[2, 7, 6] = 3.0
    return table

def dft_tables(length):
    index = jnp.arange(length, dtype=jnp.int32)
    product = index[:, None] * index[None, :] % length
    angle = product.astype(jnp.float32) * (2.0 * math.pi / length)
    factor = 1.0 / math.sqrt(length)
    return ((jnp.cos(angle) * factor).astype(jnp.bfloat16), (jnp.sin(angle) * factor).astype(jnp.bfloat16))

def monomials(wave_x, wave_y, wave_z):
    square = wave_x * wave_x + wave_y * wave_y + wave_z * wave_z
    ones = jnp.ones_like(square)
    return jnp.stack([ones, wave_x * wave_x / square, wave_y * wave_y / square, wave_z * wave_z / square, wave_x * wave_y / square, wave_x * wave_z / square, wave_y * wave_z / square])

def bin_cells(values, shell_ids, mu_ids):
    cells = values.shape[1]
    block = math.gcd(cells, 32768)
    blocks = cells // block
    value_blocks = values.reshape(3, blocks, block).transpose(1, 0, 2)
    shell_blocks = shell_ids.reshape(blocks, block)
    mu_blocks = mu_ids.reshape(blocks, block)

    def step(total, pieces):
        value_piece, shell_piece, mu_piece = pieces
        mu_hot = (mu_piece[None, :] == jnp.arange(MUBINS, dtype=jnp.int32)[:, None]).astype(jnp.float32)
        rows = (value_piece[:, None, :] * mu_hot[None]).reshape(3 * MUBINS, block)
        rows = jnp.concatenate([rows, mu_hot], axis=0)
        shell_hot = (shell_piece[None, :] == jnp.arange(SHELLS, dtype=jnp.int32)[:, None]).astype(jnp.float32)
        return (total + lax.dot_general(rows, shell_hot, (((1,), (1,)), ((), ())), precision=lax.Precision.HIGHEST), None)
    start = jnp.zeros((4 * MUBINS, SHELLS), jnp.float32)
    total, _ = lax.scan(step, start, (value_blocks, shell_blocks, mu_blocks))
    return total

def reference(fields, shells, mubins):
    group = FIELDS // N_FIELD
    cos_table, sin_table = dft_tables(NZ)
    cos_wide = cos_table.astype(jnp.float32)
    sin_wide = sin_table.astype(jnp.float32)
    coef = jnp.asarray(make_coef())
    depth = jnp.arange(NZ, dtype=jnp.int32)
    wave_z = jnp.where(depth >= NZ // 2, depth - NZ, depth).astype(jnp.float32)
    wave_y = (NZ // 8 + jnp.arange(YROWS, dtype=jnp.int32)).astype(jnp.float32)

    def plane(total, plane_index):
        data = lax.dynamic_index_in_dim(fields, plane_index, 3, keepdims=False)
        flat = data.astype(jnp.float32).reshape(NZ, 2 * FIELDS * YROWS)
        first = jnp.dot(cos_wide, flat, precision=lax.Precision.HIGHEST).reshape(NZ, 2, FIELDS, YROWS)
        second = jnp.dot(sin_wide, flat, precision=lax.Precision.HIGHEST).reshape(NZ, 2, FIELDS, YROWS)
        real_part = first[:, 0] + second[:, 1]
        imag_part = first[:, 1] - second[:, 0]
        cross = real_part[:, :1] * real_part + imag_part[:, :1] * imag_part
        wave_x = (NZ // 4 + plane_index).astype(jnp.float32)
        terms = monomials(wave_x + jnp.zeros((NZ, YROWS), jnp.float32), wave_y[None, :], wave_z[:, None])
        weights = jnp.einsum('maj,jzy->mazy', coef, terms, precision=lax.Precision.HIGHEST)
        contrib = weights * jnp.transpose(cross, (1, 0, 2))[None]
        per_group = contrib.reshape(3, N_FIELD, group, NZ, YROWS).sum(axis=2)
        rounded = lax.optimization_barrier(per_group.astype(jnp.bfloat16)).astype(jnp.float32)
        cell_values = rounded.sum(axis=1).reshape(3, NZ * YROWS)
        shell_ids = lax.dynamic_index_in_dim(shells, plane_index, 1, keepdims=False).reshape(NZ * YROWS)
        mu_ids = lax.dynamic_index_in_dim(mubins, plane_index, 1, keepdims=False).reshape(NZ * YROWS)
        return (total + bin_cells(cell_values, shell_ids, mu_ids), None)
    start = jnp.zeros((4 * MUBINS, SHELLS), jnp.float32)
    total, _ = lax.scan(plane, start, jnp.arange(PLANES, dtype=jnp.int32))
    sums = total[:3 * MUBINS].reshape(3, MUBINS, SHELLS)
    counts = total[3 * MUBINS:]
    return sums / jnp.maximum(counts, 1.0)[None]
```

```python
import functools
import math

import jax
import jax.numpy as jnp
import numpy as np
from jax import lax
from jax.experimental import pallas as pl
from jax.experimental.pallas import tpu as pltpu
from jax.sharding import PartitionSpec as P

SHELLS = 256
MUBINS = 8
LANES = 128
LOW = 16
ROWS = 5
PAIRS = 8


def quarter_tables(length, zero):
    quarter, half = length // 4, length // 2
    shape = (2, quarter, half)
    parity = lax.broadcasted_iota(jnp.int32, shape, 0)
    row = lax.broadcasted_iota(jnp.int32, shape, 1) + zero
    column = lax.broadcasted_iota(jnp.int32, shape, 2)
    depth = 2 * column + parity
    unit = 2.0 * math.pi / length
    factor = 1.0 / math.sqrt(length)
    cos_part = jnp.cos((row * depth % length).astype(jnp.float32) * unit) * factor
    sin_row = jnp.where(row == 0, quarter, row)
    sin_part = jnp.sin((sin_row * depth % length).astype(jnp.float32) * unit) * factor
    alternate = (1 - 2 * (column % 2)).astype(jnp.float32) * factor
    sin_part = jnp.where((row == 0) & (parity == 0), alternate, sin_part)
    return jnp.concatenate(
        [cos_part.astype(jnp.bfloat16), sin_part.astype(jnp.bfloat16)], axis=1
    )


def round16(value):
    return value.astype(jnp.bfloat16).astype(jnp.float32)


def kernel(length, table_ref, lines_ref, keys_ref, wave_ref, out_ref, prod, vals):
    group, parity = pl.program_id(0), pl.program_id(1)
    quarter = length // 4
    half = length // 2
    right = lines_ref[0, :, 0].reshape(half, lines_ref.shape[-1])

    def product(i, carry):
        rows = pl.ds(pl.multiple_of(i * 256, 256), 256)
        prod[group, parity, rows, :] = jnp.dot(
            table_ref[0, rows, :], right, preferred_element_type=jnp.float32
        )
        return carry

    lax.fori_loop(0, half // 256, product, 0)

    @pl.when((group == pl.num_programs(0) - 1) & (parity == 1))
    def _():
        groups, local = prod.shape[0], prod.shape[3] // (2 * LANES)
        fields = groups * local
        out_ref[...] = jnp.zeros_like(out_ref)
        wave_x = wave_ref[0:1, :]
        wave_y = wave_ref[1:2, :]
        low_iota = lax.broadcasted_iota(jnp.int32, (16, LANES), 0).astype(jnp.float32)
        iotas = [(low_iota + 16.0 * j).astype(jnp.bfloat16) for j in range(LANES // 16)]
        one = jnp.ones((16, LANES), jnp.bfloat16)
        none = jnp.zeros((16, LANES), jnp.bfloat16)

        def tile(t, carry):
            first = pl.multiple_of(t * 8, 8)
            row = lax.broadcasted_iota(jnp.int32, (8, LANES), 0) + first
            special = row == 0

            def load(a, c, parity, sine):
                g, i = a // local, a % local
                at = (c * local + i) * LANES
                return prod[g, parity, pl.ds(sine * quarter + first, 8), at : at + LANES]

            def spectra(a):
                parts = []
                for c in range(2):
                    ec, oc = load(a, c, 0, 0), load(a, c, 1, 0)
                    es, os = load(a, c, 0, 1), load(a, c, 1, 1)
                    p, q, m, n = ec + oc, es + os, ec - oc, os - es
                    parts.append(
                        (
                            (p, jnp.where(special, 0.0, q)),
                            (m, jnp.where(special, 0.0, n)),
                            (jnp.where(special, es, m), jnp.where(special, os, -n)),
                            (jnp.where(special, es, p), jnp.where(special, -os, -q)),
                        )
                    )
                u, v = parts
                return [(u[j][0] + v[j][1], v[j][0] - u[j][1]) for j in range(4)]

            k = row.astype(jnp.float32)
            zero_wave = (0.0, -half, quarter, -quarter)
            waves = (k, half - k, k - half, -k)
            base = spectra(0)
            second = None
            totals = [None] * 4
            saved = [None] * 4
            pending = [None] * 4
            for a in range(fields):
                spec = base if a == 0 else spectra(a)
                for j in range(4):
                    cross = base[j][0] * spec[j][0] + base[j][1] * spec[j][1]
                    if a == 0:
                        wz = jnp.where(special, float(zero_wave[j]), waves[j])
                        square = wave_x * wave_x + wave_y * wave_y + wz * wz
                        saved[j] = (wz, 1.0 / square)
                        vals[0, j * 8 : j * 8 + 8] = round16(cross)
                        continue
                    wz, inverse = saved[j]
                    if a == 1:
                        vals[1, j * 8 : j * 8 + 8] = round16(cross)
                        term = -0.5 * cross
                    else:
                        weight = (
                            1.5 * wave_x * wave_x,
                            1.5 * wave_y * wave_y,
                            1.5 * wz * wz,
                            3.0 * wave_x * wave_y,
                            3.0 * wave_x * wz,
                            3.0 * wave_y * wz,
                        )[a - 2]
                        term = weight * inverse * cross
                    pending[j] = term if pending[j] is None else pending[j] + term
                    if a % local == local - 1:
                        rounded = round16(pending[j])
                        totals[j] = rounded if totals[j] is None else totals[j] + rounded
                        pending[j] = None
            for j in range(4):
                high = round16(totals[j])
                vals[2, j * 8 : j * 8 + 8] = high
                vals[3, j * 8 : j * 8 + 8] = totals[j] - high
                key = keys_ref[j, pl.ds(first, 8), :]
                upper = key // LOW
                vals[4, j * 8 : j * 8 + 8] = (key - upper * LOW).astype(jnp.float32)
                vals[5, j * 8 : j * 8 + 8] = upper.astype(jnp.float32)
            total = out_ref[...]
            for start in range(0, 32, PAIRS):
                left, hot = [], []
                for r in range(start, start + PAIRS):
                    spread = [
                        jnp.broadcast_to(vals[i, r : r + 1], (16, LANES)).astype(jnp.bfloat16)
                        for i in range(6)
                    ]
                    match = spread[4] == iotas[0]
                    left.append(
                        jnp.concatenate(
                            [jnp.where(match, spread[i], none) for i in range(4)]
                            + [jnp.where(match, one, none)],
                            axis=0,
                        )
                    )
                    hot.append(
                        jnp.concatenate(
                            [jnp.where(spread[5] == it, one, none) for it in iotas], axis=0
                        )
                    )
                total = total + lax.dot_general(
                    jnp.concatenate(left, axis=1),
                    jnp.concatenate(hot, axis=1),
                    (((1,), (1,)), ((), ())),
                    preferred_element_type=jnp.float32,
                )
            out_ref[...] = total
            return carry

        lax.fori_loop(0, quarter // 8, tile, 0)


def body(fields, shells, mubins):
    depth_local, _, local_fields, planes, yrows = fields.shape
    gz_count, field_count = lax.axis_size("gz"), lax.axis_size("field")
    devices = gz_count * field_count
    length = depth_local * gz_count
    half, quarter = length // 2, length // 4
    plane_rows = planes * yrows
    width = plane_rows // devices
    me_gz, me_field = lax.axis_index("gz"), lax.axis_index("field")

    share = plane_rows // field_count
    packed = shells + mubins * 65536
    packed = lax.dynamic_slice_in_dim(
        packed.reshape(depth_local, plane_rows), me_field * share, share, 1
    )
    packed = packed.reshape(depth_local, gz_count, width).transpose(1, 0, 2)
    packed = lax.all_to_all(packed, "gz", split_axis=0, concat_axis=0, tiled=True)
    packed = packed.reshape(length, width)
    keys = (packed & 65535) * MUBINS + packed // 65536
    if width < LANES:
        keys = jnp.pad(keys, ((0, 0), (0, LANES - width)), constant_values=SHELLS * MUBINS)
    keys = jnp.stack(
        [
            keys[:quarter],
            jnp.flip(keys[quarter + 1 : half + 1], 0),
            jnp.concatenate([keys[quarter : quarter + 1], keys[half + 1 : half + quarter]], 0),
            jnp.concatenate(
                [keys[half + quarter : half + quarter + 1], jnp.flip(keys[half + quarter + 1 :], 0)],
                0,
            ),
        ]
    )

    lines = fields.reshape(depth_local // 2, 2, 2, local_fields, devices, width)
    lines = lines.transpose(4, 1, 0, 2, 3, 5).reshape(
        devices, 2, depth_local // 2, 2 * local_fields * width
    )
    lines = lax.all_to_all(lines, ("field", "gz"), split_axis=0, concat_axis=0, tiled=True)
    lines = lines.reshape(field_count, gz_count, 2, depth_local // 2, 2 * local_fields, width)
    if width < LANES:
        lines = jnp.pad(lines, ((0, 0),) * 5 + ((0, LANES - width),))
    span = 2 * local_fields * LANES
    lines = lines.reshape(field_count, gz_count, 2, depth_local // 2, span)

    table = quarter_tables(length, jnp.minimum(me_gz, 0))
    column = (me_field * gz_count + me_gz) * width + jnp.arange(LANES, dtype=jnp.int32)
    waves = jnp.stack([length // 4 + column // yrows, length // 8 + column % yrows])
    waves = jnp.pad(waves.astype(jnp.float32), ((0, 6), (0, 0)))

    total = pl.pallas_call(
        functools.partial(kernel, length),
        grid=(field_count, 2),
        out_shape=jax.ShapeDtypeStruct((ROWS * LOW, LANES), jnp.float32),
        in_specs=[
            pl.BlockSpec((1, half, half), lambda f, p: (p, 0, 0)),
            pl.BlockSpec(
                (1, gz_count, 1, depth_local // 2, span), lambda f, p: (f, 0, p, 0, 0)
            ),
            pl.BlockSpec((4, quarter, LANES), lambda f, p: (0, 0, 0)),
            pl.BlockSpec((8, LANES), lambda f, p: (0, 0)),
        ],
        out_specs=pl.BlockSpec((ROWS * LOW, LANES), lambda f, p: (0, 0)),
        scratch_shapes=[
            pltpu.VMEM((field_count, 2, half, span), jnp.float32),
            pltpu.VMEM((6, 32, LANES), jnp.float32),
        ],
        compiler_params=pltpu.CompilerParams(vmem_limit_bytes=48 * 1024 * 1024),
    )(table, lines, keys, waves)

    total = lax.psum(total, ("field", "gz"))
    total = total.reshape(ROWS, 2, MUBINS, LANES).transpose(0, 2, 3, 1)
    total = total.reshape(ROWS, MUBINS, SHELLS)
    sums = jnp.stack([total[0], total[1], total[2] + total[3]])
    return sums / jnp.maximum(total[4], 1.0)[None]


def solution(mesh):
    in_specs = (P("gz", None, "field", None, None), P("gz", None, None), P("gz", None, None))
    return jax.shard_map(body, mesh=mesh, in_specs=in_specs, out_specs=P(), check_vma=False)
```

```python
import functools
import math

import jax
import jax.numpy as jnp
import numpy as np
from jax import lax
from jax.experimental import pallas as pl
from jax.experimental.pallas import tpu as pltpu
from jax.sharding import PartitionSpec as P

SHELLS = 256
MUBINS = 8
LANES = 128
LOW = 16
ROWS = 5
PAIRS = 8


def quarter_tables(length, zero):
    quarter, half = length // 4, length // 2
    shape = (2, quarter, half)
    parity = lax.broadcasted_iota(jnp.int32, shape, 0)
    row = lax.broadcasted_iota(jnp.int32, shape, 1) + zero
    column = lax.broadcasted_iota(jnp.int32, shape, 2)
    depth = 2 * column + parity
    unit = 2.0 * math.pi / length
    factor = 1.0 / math.sqrt(length)
    cos_part = jnp.cos((row * depth % length).astype(jnp.float32) * unit) * factor
    sin_row = jnp.where(row == 0, quarter, row)
    sin_part = jnp.sin((sin_row * depth % length).astype(jnp.float32) * unit) * factor
    alternate = (1 - 2 * (column % 2)).astype(jnp.float32) * factor
    sin_part = jnp.where((row == 0) & (parity == 0), alternate, sin_part)
    return jnp.concatenate(
        [cos_part.astype(jnp.bfloat16), sin_part.astype(jnp.bfloat16)], axis=1
    )


def round16(value):
    return value.astype(jnp.bfloat16).astype(jnp.float32)


def kernel(length, table_ref, lines_ref, keys_ref, wave_ref, out_ref, prod, vals):
    group, parity = pl.program_id(0), pl.program_id(1)
    quarter = length // 4
    half = length // 2
    right = lines_ref[0, :, 0].reshape(half, lines_ref.shape[-1])

    def product(i, carry):
        rows = pl.ds(pl.multiple_of(i * 256, 256), 256)
        prod[group, parity, rows, :] = jnp.dot(
            table_ref[0, rows, :], right, preferred_element_type=jnp.float32
        )
        return carry

    lax.fori_loop(0, half // 256, product, 0)

    @pl.when((group == pl.num_programs(0) - 1) & (parity == 1))
    def _():
        groups, local = prod.shape[0], prod.shape[3] // (2 * LANES)
        fields = groups * local
        out_ref[...] = jnp.zeros_like(out_ref)
        wave_x = wave_ref[0:1, :]
        wave_y = wave_ref[1:2, :]
        low_iota = lax.broadcasted_iota(jnp.int32, (16, LANES), 0).astype(jnp.float32)
        iotas = [(low_iota + 16.0 * j).astype(jnp.bfloat16) for j in range(LANES // 16)]
        one = jnp.ones((16, LANES), jnp.bfloat16)
        none = jnp.zeros((16, LANES), jnp.bfloat16)

        def tile(t, carry):
            first = pl.multiple_of(t * 8, 8)
            row = lax.broadcasted_iota(jnp.int32, (8, LANES), 0) + first
            special = row == 0

            def load(a, c, parity, sine):
                g, i = a // local, a % local
                at = (c * local + i) * LANES
                return prod[g, parity, pl.ds(sine * quarter + first, 8), at : at + LANES]

            def spectra(a):
                parts = []
                for c in range(2):
                    ec, oc = load(a, c, 0, 0), load(a, c, 1, 0)
                    es, os = load(a, c, 0, 1), load(a, c, 1, 1)
                    p, q, m, n = ec + oc, es + os, ec - oc, os - es
                    parts.append(
                        (
                            (p, jnp.where(special, 0.0, q)),
                            (m, jnp.where(special, 0.0, n)),
                            (jnp.where(special, es, m), jnp.where(special, os, -n)),
                            (jnp.where(special, es, p), jnp.where(special, -os, -q)),
                        )
                    )
                u, v = parts
                return [(u[j][0] + v[j][1], v[j][0] - u[j][1]) for j in range(4)]

            k = row.astype(jnp.float32)
            zero_wave = (0.0, -half, quarter, -quarter)
            waves = (k, half - k, k - half, -k)
            base = spectra(0)
            second = None
            totals = [None] * 4
            saved = [None] * 4
            pending = [None] * 4
            for a in range(fields):
                spec = base if a == 0 else spectra(a)
                for j in range(4):
                    cross = base[j][0] * spec[j][0] + base[j][1] * spec[j][1]
                    if a == 0:
                        wz = jnp.where(special, float(zero_wave[j]), waves[j])
                        square = wave_x * wave_x + wave_y * wave_y + wz * wz
                        saved[j] = (wz, 1.0 / square)
                        vals[0, j * 8 : j * 8 + 8] = round16(cross)
                        continue
                    wz, inverse = saved[j]
                    if a == 1:
                        vals[1, j * 8 : j * 8 + 8] = round16(cross)
                        term = -0.5 * cross
                    else:
                        weight = (
                            1.5 * wave_x * wave_x,
                            1.5 * wave_y * wave_y,
                            1.5 * wz * wz,
                            3.0 * wave_x * wave_y,
                            3.0 * wave_x * wz,
                            3.0 * wave_y * wz,
                        )[a - 2]
                        term = weight * inverse * cross
                    pending[j] = term if pending[j] is None else pending[j] + term
                    if a % local == local - 1:
                        rounded = round16(pending[j])
                        totals[j] = rounded if totals[j] is None else totals[j] + rounded
                        pending[j] = None
            for j in range(4):
                high = round16(totals[j])
                vals[2, j * 8 : j * 8 + 8] = high
                vals[3, j * 8 : j * 8 + 8] = totals[j] - high
                key = keys_ref[j, pl.ds(first, 8), :]
                upper = key // LOW
                vals[4, j * 8 : j * 8 + 8] = (key - upper * LOW).astype(jnp.float32)
                vals[5, j * 8 : j * 8 + 8] = upper.astype(jnp.float32)
            total = out_ref[...]
            for start in range(0, 32, PAIRS):
                left, hot = [], []
                for r in range(start, start + PAIRS):
                    spread = [
                        jnp.broadcast_to(vals[i, r : r + 1], (16, LANES)).astype(jnp.bfloat16)
                        for i in range(6)
                    ]
                    match = spread[4] == iotas[0]
                    left.append(
                        jnp.concatenate(
                            [jnp.where(match, spread[i], none) for i in range(4)]
                            + [jnp.where(match, one, none)],
                            axis=0,
                        )
                    )
                    hot.append(
                        jnp.concatenate(
                            [jnp.where(spread[5] == it, one, none) for it in iotas], axis=0
                        )
                    )
                total = total + lax.dot_general(
                    jnp.concatenate(left, axis=1),
                    jnp.concatenate(hot, axis=1),
                    (((1,), (1,)), ((), ())),
                    preferred_element_type=jnp.float32,
                )
            out_ref[...] = total
            return carry

        lax.fori_loop(0, quarter // 8, tile, 0)


def relayout_kernel(fields_ref, out_ref):
    for c in range(2):
        for i in range(fields_ref.shape[2]):
            at = (c * fields_ref.shape[2] + i) * LANES
            for h in range(out_ref.shape[1]):
                block = fields_ref[:, c, i, :, h * LANES : (h + 1) * LANES]
                block = block.reshape(16, 2, block.shape[1], LANES)
                for parity in range(2):
                    out_ref[:, h, parity, :, at : at + LANES] = jnp.swapaxes(
                        block[:, parity], 0, 1
                    )


def relayout(fields):
    depth, _, local, planes, yrows = fields.shape
    parts = yrows // LANES
    out = pl.pallas_call(
        relayout_kernel,
        grid=(depth // 32,),
        out_shape=jax.ShapeDtypeStruct(
            (planes, parts, 2, depth // 2, 2 * local * LANES), fields.dtype
        ),
        in_specs=[pl.BlockSpec((32, 2, local, planes, yrows), lambda i: (i, 0, 0, 0, 0))],
        out_specs=pl.BlockSpec(
            (planes, parts, 2, 16, 2 * local * LANES), lambda i: (0, 0, 0, i, 0)
        ),
    )(fields)
    return out.reshape(planes * parts, 2, depth // 2, 2 * local * LANES)


def reduce_kernel(field_count, gz_count, mine_ref, out_ref, parts, answer, send, recv, send2, recv2):
    devices = field_count * gz_count
    me_field, me_gz = lax.axis_index("field"), lax.axis_index("gz")
    me = me_field * gz_count + me_gz

    def peer(step):
        other = lax.rem(me + step, devices)
        return other, (other // gz_count, lax.rem(other, gz_count))

    barrier = pltpu.get_barrier_semaphore()

    def greet(step, carry):
        _, place = peer(step)
        pl.semaphore_signal(
            barrier, inc=1, device_id=place, device_id_type=pl.DeviceIdType.MESH
        )
        return carry

    lax.fori_loop(1, devices, greet, 0)
    pl.semaphore_wait(barrier, devices - 1)

    def scatter(step):
        other, place = peer(step)
        return pltpu.make_async_remote_copy(
            src_ref=mine_ref.at[other],
            dst_ref=parts.at[step],
            send_sem=send.at[step],
            recv_sem=recv.at[step],
            device_id=place,
            device_id_type=pl.DeviceIdType.MESH,
        )

    def gather(step):
        _, place = peer(step)
        return pltpu.make_async_remote_copy(
            src_ref=answer,
            dst_ref=out_ref.at[me],
            send_sem=send2.at[step],
            recv_sem=recv2.at[step],
            device_id=place,
            device_id_type=pl.DeviceIdType.MESH,
        )

    def start(copy):
        def run(step, carry):
            copy(step).start()
            return carry

        lax.fori_loop(1, devices, run, 0)

    start(scatter)

    def collect(step, total):
        scatter(step).wait_recv()
        return total + parts[step]

    answer[...] = lax.fori_loop(1, devices, collect, mine_ref[me])
    start(gather)
    out_ref[me] = answer[...]

    def finish(step, carry):
        scatter(step).wait_send()
        gather(step).wait()
        return carry

    lax.fori_loop(1, devices, finish, 0)


def all_reduce(total, field_count, gz_count):
    devices = field_count * gz_count
    rows = max(1, total.shape[0] // devices)
    total = jnp.pad(total, ((0, devices * rows - total.shape[0]), (0, 0)))
    total = total.reshape(devices, rows, LANES)
    return pl.pallas_call(
        functools.partial(reduce_kernel, field_count, gz_count),
        out_shape=jax.ShapeDtypeStruct(total.shape, jnp.float32),
        in_specs=[pl.BlockSpec(memory_space=pltpu.VMEM)],
        out_specs=pl.BlockSpec(memory_space=pltpu.VMEM),
        scratch_shapes=[
            pltpu.VMEM(total.shape, jnp.float32),
            pltpu.VMEM(total.shape[1:], jnp.float32),
            pltpu.SemaphoreType.DMA((devices,)),
            pltpu.SemaphoreType.DMA((devices,)),
            pltpu.SemaphoreType.DMA((devices,)),
            pltpu.SemaphoreType.DMA((devices,)),
        ],
        compiler_params=pltpu.CompilerParams(collective_id=0, has_side_effects=True),
    )(total).reshape(devices * rows, LANES)


def body(fields, shells, mubins):
    depth_local, _, local_fields, planes, yrows = fields.shape
    gz_count, field_count = lax.axis_size("gz"), lax.axis_size("field")
    devices = gz_count * field_count
    length = depth_local * gz_count
    half, quarter = length // 2, length // 4
    plane_rows = planes * yrows
    width = plane_rows // devices
    me_gz, me_field = lax.axis_index("gz"), lax.axis_index("field")

    if width == LANES and depth_local % 32 == 0:
        lines = relayout(fields)
    else:
        lines = fields.reshape(depth_local // 2, 2, 2, local_fields, devices, width)
        lines = lines.transpose(4, 1, 0, 2, 3, 5).reshape(
            devices, 2, depth_local // 2, 2 * local_fields * width
        )
    lines, shells, mubins = lax.optimization_barrier((lines, shells, mubins))

    share = plane_rows // field_count
    packed = shells + mubins * 65536
    packed = lax.dynamic_slice_in_dim(
        packed.reshape(depth_local, plane_rows), me_field * share, share, 1
    )
    packed = packed.reshape(depth_local, gz_count, width).transpose(1, 0, 2)
    packed = lax.all_to_all(packed, "gz", split_axis=0, concat_axis=0, tiled=True)
    packed = packed.reshape(length, width)
    keys = (packed & 65535) * MUBINS + packed // 65536
    if width < LANES:
        keys = jnp.pad(keys, ((0, 0), (0, LANES - width)), constant_values=SHELLS * MUBINS)
    keys = jnp.stack(
        [
            keys[:quarter],
            jnp.flip(keys[quarter + 1 : half + 1], 0),
            jnp.concatenate([keys[quarter : quarter + 1], keys[half + 1 : half + quarter]], 0),
            jnp.concatenate(
                [keys[half + quarter : half + quarter + 1], jnp.flip(keys[half + quarter + 1 :], 0)],
                0,
            ),
        ]
    )

    lines = lax.all_to_all(lines, ("field", "gz"), split_axis=0, concat_axis=0, tiled=True)
    lines = lines.reshape(field_count, gz_count, 2, depth_local // 2, 2 * local_fields, width)
    if width < LANES:
        lines = jnp.pad(lines, ((0, 0),) * 5 + ((0, LANES - width),))
    span = 2 * local_fields * LANES
    lines = lines.reshape(field_count, gz_count, 2, depth_local // 2, span)

    table = quarter_tables(length, jnp.minimum(me_gz, 0))
    column = (me_field * gz_count + me_gz) * width + jnp.arange(LANES, dtype=jnp.int32)
    waves = jnp.stack([length // 4 + column // yrows, length // 8 + column % yrows])
    waves = jnp.pad(waves.astype(jnp.float32), ((0, 6), (0, 0)))

    total = pl.pallas_call(
        functools.partial(kernel, length),
        grid=(field_count, 2),
        out_shape=jax.ShapeDtypeStruct((ROWS * LOW, LANES), jnp.float32),
        in_specs=[
            pl.BlockSpec((1, half, half), lambda f, p: (p, 0, 0)),
            pl.BlockSpec(
                (1, gz_count, 1, depth_local // 2, span), lambda f, p: (f, 0, p, 0, 0)
            ),
            pl.BlockSpec((4, quarter, LANES), lambda f, p: (0, 0, 0)),
            pl.BlockSpec((8, LANES), lambda f, p: (0, 0)),
        ],
        out_specs=pl.BlockSpec((ROWS * LOW, LANES), lambda f, p: (0, 0)),
        scratch_shapes=[
            pltpu.VMEM((field_count, 2, half, span), jnp.float32),
            pltpu.VMEM((6, 32, LANES), jnp.float32),
        ],
        compiler_params=pltpu.CompilerParams(vmem_limit_bytes=48 * 1024 * 1024),
    )(table, lines, keys, waves)

    total = total.reshape(ROWS, LOW, LANES)
    total = jnp.concatenate([total[:2], total[2:3] + total[3:4], total[4:]])
    total = all_reduce(total.reshape(-1, LANES), field_count, gz_count)[: 4 * LOW]
    total = total.reshape(4, 2, MUBINS, LANES).transpose(0, 2, 3, 1)
    total = total.reshape(4, MUBINS, SHELLS)
    return total[:3] / jnp.maximum(total[3], 1.0)[None]


def solution(mesh):
    in_specs = (P("gz", None, "field", None, None), P("gz", None, None), P("gz", None, None))
    return jax.shard_map(body, mesh=mesh, in_specs=in_specs, out_specs=P(), check_vma=False)
```

```python
import functools
import math

import jax
import jax.numpy as jnp
import numpy as np
from jax import lax
from jax.experimental import pallas as pl
from jax.experimental.pallas import tpu as pltpu
from jax.sharding import PartitionSpec as P

SHELLS = 256
MUBINS = 8
LANES = 128
LOW = 16
ROWS = 5
PAIRS = 8


def quarter_tables(length, zero):
    quarter, half = length // 4, length // 2
    unit = 2.0 * math.pi / length
    factor = 1.0 / math.sqrt(length)

    def pair(rows, stride):
        shape = (2, rows, half)
        parity = lax.broadcasted_iota(jnp.int32, shape, 0)
        row = lax.broadcasted_iota(jnp.int32, shape, 1) * stride + zero
        depth = 2 * lax.broadcasted_iota(jnp.int32, shape, 2) + parity
        angle = (row * depth % length).astype(jnp.float32) * unit
        return jnp.cos(angle), jnp.sin(angle)

    fine = 16
    ca, sa, cb, sb = lax.optimization_barrier(pair(quarter // fine, fine) + pair(fine, 1))
    ca, sa, cb, sb = ca[:, :, None], sa[:, :, None], cb[:, None], sb[:, None]
    cos_part = ((ca * cb - sa * sb) * factor).reshape(2, quarter, half)
    sin_part = ((sa * cb + ca * sb) * factor).reshape(2, quarter, half)
    row = lax.broadcasted_iota(jnp.int32, sin_part.shape, 1)
    column = lax.broadcasted_iota(jnp.int32, sin_part.shape, 2)
    alternate = (1 - 2 * (column % 2)).astype(jnp.float32) * factor
    sin_part = jnp.where(row == 0, alternate, sin_part)
    return jnp.concatenate(
        [cos_part.astype(jnp.bfloat16), sin_part.astype(jnp.bfloat16)], axis=1
    )


def round16(value):
    return value.astype(jnp.bfloat16).astype(jnp.float32)


def unpack(index_ref, keys):
    depth = index_ref.shape[1]

    def block(g, carry):
        word = index_ref[g]
        mu = word // 65536
        key = (word - mu * 65536) * MUBINS + mu
        upper = key // LOW
        rows = pl.ds(pl.multiple_of(g * depth, depth), depth)
        keys[0, rows, :] = (key - upper * LOW).astype(jnp.float32)
        keys[1, rows, :] = upper.astype(jnp.float32)
        return carry

    lax.fori_loop(0, index_ref.shape[0], block, 0)


def products(table_ref, lines_ref, prod, parity):
    half = table_ref.shape[1]

    def group(f, carry):
        right = lines_ref[f, :, parity].reshape(half, lines_ref.shape[-1])

        def rows_of(i, inner):
            rows = pl.ds(pl.multiple_of(i * 256, 256), 256)
            prod[f, parity, rows, :] = jnp.dot(
                table_ref[parity, rows, :], right, preferred_element_type=jnp.float32
            )
            return inner

        return lax.fori_loop(0, half // 256, rows_of, carry)

    lax.fori_loop(0, prod.shape[0], group, 0)


def local_kernel(length, table_ref, lines_ref, index_ref, wave_ref, out_ref, prod, vals, keys):
    unpack(index_ref, keys)
    products(table_ref, lines_ref, prod, 0)
    products(table_ref, lines_ref, prod, 1)
    bins(length, wave_ref, out_ref, prod, vals, keys)


def exchange_kernel(
    length, field_count, gz_count, table_ref, lines_ref, index_ref, wave_ref, out_ref,
    prod, vals, keys, lines, index, send, recv, own, index_send, index_recv, index_own,
):
    devices = field_count * gz_count
    me_field, me_gz = lax.axis_index("field"), lax.axis_index("gz")
    far = gz_count // 2
    mine = (gz_count - far) * field_count

    def peer(step):
        f = lax.rem(me_field + lax.rem(step, field_count), field_count)
        g = lax.rem(me_gz + step // field_count + far, gz_count)
        return f, g

    def others(run):
        def loop(step, carry):
            run(step)
            return carry

        lax.fori_loop(0, mine, loop, 0)
        lax.fori_loop(mine + 1, devices, loop, 0)

    def along(run):
        def loop(step, carry):
            run(step)
            return carry

        lax.fori_loop(1, gz_count, loop, 0)

    barrier = pltpu.get_barrier_semaphore()
    others(
        lambda step: pl.semaphore_signal(
            barrier, inc=1, device_id=peer(step), device_id_type=pl.DeviceIdType.MESH
        )
    )
    pl.semaphore_wait(barrier, devices - 1)

    def index_copy(step):
        g = lax.rem(me_gz + step, gz_count)
        return pltpu.make_async_remote_copy(
            src_ref=index_ref.at[g],
            dst_ref=index.at[me_gz],
            send_sem=index_send.at[step],
            recv_sem=index_recv.at[step],
            device_id=(me_field, g),
            device_id_type=pl.DeviceIdType.MESH,
        )

    def lines_copy(parity):
        def copy(step):
            f, g = peer(step)
            return pltpu.make_async_remote_copy(
                src_ref=lines_ref.at[f * gz_count + g, parity],
                dst_ref=lines.at[me_field, me_gz, parity],
                send_sem=send.at[parity, step],
                recv_sem=recv.at[parity, step],
                device_id=(f, g),
                device_id_type=pl.DeviceIdType.MESH,
            )

        return copy

    along(lambda step: index_copy(step).start())
    for parity in range(2):
        others(lambda step: lines_copy(parity)(step).start())
    me = me_field * gz_count + me_gz
    kept = [
        pltpu.make_async_copy(
            lines_ref.at[me, parity], lines.at[me_field, me_gz, parity], own.at[parity]
        )
        for parity in range(2)
    ]
    kept_index = pltpu.make_async_copy(index_ref.at[me_gz], index.at[me_gz], index_own)
    for copy in kept + [kept_index]:
        copy.start()

    kept_index.wait()
    along(lambda step: index_copy(step).wait_recv())
    unpack(index, keys)
    for parity in range(2):
        kept[parity].wait()
        others(lambda step: lines_copy(parity)(step).wait_recv())
        products(table_ref, lines, prod, parity)
    bins(length, wave_ref, out_ref, prod, vals, keys)
    along(lambda step: index_copy(step).wait_send())
    for parity in range(2):
        others(lambda step: lines_copy(parity)(step).wait_send())


def bins(length, wave_ref, out_ref, prod, vals, keys):
    quarter, half = length // 4, length // 2
    groups, local = prod.shape[0], prod.shape[3] // (2 * LANES)
    fields = groups * local
    out_ref[...] = jnp.zeros_like(out_ref)
    wave_x = wave_ref[0:1, :]
    wave_y = wave_ref[1:2, :]
    low_iota = lax.broadcasted_iota(jnp.int32, (16, LANES), 0).astype(jnp.float32)
    iotas = [(low_iota + 16.0 * j).astype(jnp.bfloat16) for j in range(LANES // 16)]
    one = jnp.ones((16, LANES), jnp.bfloat16)
    none = jnp.zeros((16, LANES), jnp.bfloat16)

    def cell_row(j, k):
        start = 1 - (k + quarter - 1) // quarter
        return (
            k,
            half - k,
            half + k - quarter * start,
            length - k - quarter * start,
        )[j]

    def tile(t, carry):
        first = pl.multiple_of(t * 8, 8)
        row = lax.broadcasted_iota(jnp.int32, (8, LANES), 0) + first
        special = row == 0

        def load(a, c, parity, sine):
            g, i = a // local, a % local
            at = (c * local + i) * LANES
            return prod[g, parity, pl.ds(sine * quarter + first, 8), at : at + LANES]

        def spectra(a):
            parts = []
            for c in range(2):
                ec, oc = load(a, c, 0, 0), load(a, c, 1, 0)
                es, os = load(a, c, 0, 1), load(a, c, 1, 1)
                p, q, m, n = ec + oc, es + os, ec - oc, os - es
                parts.append(
                    (
                        (p, jnp.where(special, 0.0, q)),
                        (m, jnp.where(special, 0.0, n)),
                        (jnp.where(special, es, m), jnp.where(special, os, -n)),
                        (jnp.where(special, es, p), jnp.where(special, -os, -q)),
                    )
                )
            u, v = parts
            return [(u[j][0] + v[j][1], v[j][0] - u[j][1]) for j in range(4)]

        k = row.astype(jnp.float32)
        zero_wave = (0.0, -half, quarter, -quarter)
        waves = (k, half - k, k - half, -k)
        base = spectra(0)
        second = None
        totals = [None] * 4
        saved = [None] * 4
        pending = [None] * 4
        for a in range(fields):
            spec = base if a == 0 else spectra(a)
            for j in range(4):
                cross = base[j][0] * spec[j][0] + base[j][1] * spec[j][1]
                if a == 0:
                    wz = jnp.where(special, float(zero_wave[j]), waves[j])
                    square = wave_x * wave_x + wave_y * wave_y + wz * wz
                    saved[j] = (wz, 1.0 / square)
                    vals[0, j * 8 : j * 8 + 8] = round16(cross)
                    continue
                wz, inverse = saved[j]
                if a == 1:
                    vals[1, j * 8 : j * 8 + 8] = round16(cross)
                    term = -0.5 * cross
                else:
                    weight = (
                        1.5 * wave_x * wave_x,
                        1.5 * wave_y * wave_y,
                        1.5 * wz * wz,
                        3.0 * wave_x * wave_y,
                        3.0 * wave_x * wz,
                        3.0 * wave_y * wz,
                    )[a - 2]
                    term = weight * inverse * cross
                pending[j] = term if pending[j] is None else pending[j] + term
                if a % local == local - 1:
                    rounded = round16(pending[j])
                    totals[j] = rounded if totals[j] is None else totals[j] + rounded
                    pending[j] = None
        for j in range(4):
            high = round16(totals[j])
            vals[2, j * 8 : j * 8 + 8] = high
            vals[3, j * 8 : j * 8 + 8] = totals[j] - high
        total = out_ref[...]
        for start in range(0, 32, PAIRS):
            left, hot = [], []
            for r in range(start, start + PAIRS):
                cell = cell_row(r // 8, first + r % 8)
                spread = [
                    jnp.broadcast_to(part, (16, LANES)).astype(jnp.bfloat16)
                    for part in [vals[i, r : r + 1] for i in range(4)]
                    + [keys[i, pl.ds(cell, 1), :] for i in range(2)]
                ]
                match = spread[4] == iotas[0]
                left.append(
                    jnp.concatenate(
                        [jnp.where(match, spread[i], none) for i in range(4)]
                        + [jnp.where(match, one, none)],
                        axis=0,
                    )
                )
                hot.append(
                    jnp.concatenate(
                        [jnp.where(spread[5] == it, one, none) for it in iotas], axis=0
                    )
                )
            total = total + lax.dot_general(
                jnp.concatenate(left, axis=1),
                jnp.concatenate(hot, axis=1),
                (((1,), (1,)), ((), ())),
                preferred_element_type=jnp.float32,
            )
        out_ref[...] = total
        return carry

    lax.fori_loop(0, quarter // 8, tile, 0)


def relayout_kernel(fields_ref, out_ref):
    for c in range(2):
        for i in range(fields_ref.shape[2]):
            at = (c * fields_ref.shape[2] + i) * LANES
            for h in range(out_ref.shape[1]):
                block = fields_ref[:, c, i, :, h * LANES : (h + 1) * LANES]
                block = block.reshape(16, 2, block.shape[1], LANES)
                for parity in range(2):
                    out_ref[:, h, parity, :, at : at + LANES] = jnp.swapaxes(
                        block[:, parity], 0, 1
                    )


def relayout(fields):
    depth, _, local, planes, yrows = fields.shape
    parts = yrows // LANES
    out = pl.pallas_call(
        relayout_kernel,
        grid=(depth // 32,),
        out_shape=jax.ShapeDtypeStruct(
            (planes, parts, 2, depth // 2, 2 * local * LANES), fields.dtype
        ),
        in_specs=[pl.BlockSpec((32, 2, local, planes, yrows), lambda i: (i, 0, 0, 0, 0))],
        out_specs=pl.BlockSpec(
            (planes, parts, 2, 16, 2 * local * LANES), lambda i: (0, 0, 0, i, 0)
        ),
    )(fields)
    return out.reshape(planes * parts, 2, depth // 2, 2 * local * LANES)


def reduce_kernel(field_count, gz_count, mine_ref, out_ref, parts, answer, send, recv, send2, recv2):
    devices = field_count * gz_count
    me_field, me_gz = lax.axis_index("field"), lax.axis_index("gz")
    me = me_field * gz_count + me_gz

    def peer(step):
        other = lax.rem(me + step, devices)
        return other, (other // gz_count, lax.rem(other, gz_count))

    barrier = pltpu.get_barrier_semaphore()

    def greet(step, carry):
        _, place = peer(step)
        pl.semaphore_signal(
            barrier, inc=1, device_id=place, device_id_type=pl.DeviceIdType.MESH
        )
        return carry

    lax.fori_loop(1, devices, greet, 0)
    pl.semaphore_wait(barrier, devices - 1)

    def scatter(step):
        other, place = peer(step)
        return pltpu.make_async_remote_copy(
            src_ref=mine_ref.at[other],
            dst_ref=parts.at[step],
            send_sem=send.at[step],
            recv_sem=recv.at[step],
            device_id=place,
            device_id_type=pl.DeviceIdType.MESH,
        )

    def gather(step):
        _, place = peer(step)
        return pltpu.make_async_remote_copy(
            src_ref=answer,
            dst_ref=out_ref.at[me],
            send_sem=send2.at[step],
            recv_sem=recv2.at[step],
            device_id=place,
            device_id_type=pl.DeviceIdType.MESH,
        )

    def start(copy):
        def run(step, carry):
            copy(step).start()
            return carry

        lax.fori_loop(1, devices, run, 0)

    start(scatter)

    def collect(step, total):
        scatter(step).wait_recv()
        return total + parts[step]

    answer[...] = lax.fori_loop(1, devices, collect, mine_ref[me])
    start(gather)
    out_ref[me] = answer[...]

    def finish(step, carry):
        scatter(step).wait_send()
        gather(step).wait()
        return carry

    lax.fori_loop(1, devices, finish, 0)


def all_reduce(total, field_count, gz_count):
    devices = field_count * gz_count
    rows = max(1, total.shape[0] // devices)
    total = jnp.pad(total, ((0, devices * rows - total.shape[0]), (0, 0)))
    total = total.reshape(devices, rows, LANES)
    return pl.pallas_call(
        functools.partial(reduce_kernel, field_count, gz_count),
        out_shape=jax.ShapeDtypeStruct(total.shape, jnp.float32),
        in_specs=[pl.BlockSpec(memory_space=pltpu.VMEM)],
        out_specs=pl.BlockSpec(memory_space=pltpu.VMEM),
        scratch_shapes=[
            pltpu.VMEM(total.shape, jnp.float32),
            pltpu.VMEM(total.shape[1:], jnp.float32),
            pltpu.SemaphoreType.DMA((devices,)),
            pltpu.SemaphoreType.DMA((devices,)),
            pltpu.SemaphoreType.DMA((devices,)),
            pltpu.SemaphoreType.DMA((devices,)),
        ],
        compiler_params=pltpu.CompilerParams(collective_id=0, has_side_effects=True),
    )(total).reshape(devices * rows, LANES)


def body(fields, shells, mubins):
    depth_local, _, local_fields, planes, yrows = fields.shape
    gz_count, field_count = lax.axis_size("gz"), lax.axis_size("field")
    devices = gz_count * field_count
    length = depth_local * gz_count
    half = length // 2
    plane_rows = planes * yrows
    width = plane_rows // devices
    me_gz, me_field = lax.axis_index("gz"), lax.axis_index("field")

    exchange = width == LANES and depth_local % 32 == 0
    if exchange:
        lines = relayout(fields)
    else:
        lines = fields.reshape(depth_local // 2, 2, 2, local_fields, devices, width)
        lines = lines.transpose(4, 1, 0, 2, 3, 5).reshape(
            devices, 2, depth_local // 2, 2 * local_fields * width
        )

    share = planes // field_count
    shells, mubins = (
        lax.dynamic_slice_in_dim(ids, me_field * share, share, 1) for ids in (shells, mubins)
    )
    index = (shells + mubins * 65536).reshape(depth_local, gz_count, width).transpose(1, 0, 2)

    span = 2 * local_fields * LANES
    table = quarter_tables(length, jnp.minimum(me_gz, 0))
    column = (me_field * gz_count + me_gz) * width + jnp.arange(LANES, dtype=jnp.int32)
    waves = jnp.stack([length // 4 + column // yrows, length // 8 + column % yrows])
    waves = jnp.pad(waves.astype(jnp.float32), ((0, 6), (0, 0)))
    landed = (field_count, gz_count, 2, depth_local // 2, span)
    scratch = [
        pltpu.VMEM((field_count, 2, half, span), jnp.float32),
        pltpu.VMEM((4, 32, LANES), jnp.float32),
        pltpu.VMEM((2, length, LANES), jnp.float32),
    ]
    vmem, anywhere = pl.BlockSpec(memory_space=pltpu.VMEM), pl.BlockSpec(memory_space=pl.ANY)
    if exchange:
        run, places, wide = (
            functools.partial(exchange_kernel, length, field_count, gz_count),
            anywhere,
            dict(collective_id=1, has_side_effects=True),
        )
        scratch += [
            pltpu.VMEM(landed, jnp.bfloat16),
            pltpu.VMEM((gz_count, depth_local, LANES), jnp.int32),
            pltpu.SemaphoreType.DMA((2, devices)),
            pltpu.SemaphoreType.DMA((2, devices)),
            pltpu.SemaphoreType.DMA((2,)),
            pltpu.SemaphoreType.DMA((gz_count,)),
            pltpu.SemaphoreType.DMA((gz_count,)),
            pltpu.SemaphoreType.DMA,
        ]
    else:
        run, places, wide = functools.partial(local_kernel, length), vmem, {}
        lines = lax.all_to_all(lines, ("field", "gz"), split_axis=0, concat_axis=0, tiled=True)
        lines = lines.reshape(landed[:-1] + (2 * local_fields, width))
        lines = jnp.pad(lines, ((0, 0),) * 5 + ((0, LANES - width),)).reshape(landed)
        index = lax.all_to_all(index, "gz", split_axis=0, concat_axis=0, tiled=True)
        index = jnp.pad(index, ((0, 0), (0, 0), (0, LANES - width)), constant_values=SHELLS)

    total = pl.pallas_call(
        run,
        out_shape=jax.ShapeDtypeStruct((ROWS * LOW, LANES), jnp.float32),
        in_specs=[vmem, places, places, vmem],
        out_specs=vmem,
        scratch_shapes=scratch,
        compiler_params=pltpu.CompilerParams(vmem_limit_bytes=56 * 1024 * 1024, **wide),
    )(table, lines, index, waves)

    total = total.reshape(ROWS, LOW, LANES)
    total = jnp.concatenate([total[:2], total[2:3] + total[3:4], total[4:]])
    total = all_reduce(total.reshape(-1, LANES), field_count, gz_count)[: 4 * LOW]
    total = total.reshape(4, 2, MUBINS, LANES).transpose(0, 2, 3, 1)
    total = total.reshape(4, MUBINS, SHELLS)
    return total[:3] / jnp.maximum(total[3], 1.0)[None]


def solution(mesh):
    in_specs = (P("gz", None, "field", None, None), P("gz", None, None), P("gz", None, None))
    return jax.shard_map(body, mesh=mesh, in_specs=in_specs, out_specs=P(), check_vma=False)
```

```python
import functools
import math

import jax
import jax.numpy as jnp
import numpy as np
from jax import lax
from jax.experimental import pallas as pl
from jax.experimental.pallas import tpu as pltpu
from jax.sharding import PartitionSpec as P

SHELLS = 256
MUBINS = 8
LANES = 128
LOW = 16
ROWS = 5
PAIRS = 32


def quarter_tables(length, zero):
    quarter, half = length // 4, length // 2
    unit = 2.0 * math.pi / length
    factor = 1.0 / math.sqrt(length)

    def pair(rows, stride):
        shape = (2, rows, half)
        parity = lax.broadcasted_iota(jnp.int32, shape, 0)
        row = lax.broadcasted_iota(jnp.int32, shape, 1) * stride + zero
        depth = 2 * lax.broadcasted_iota(jnp.int32, shape, 2) + parity
        angle = (row * depth % length).astype(jnp.float32) * unit
        return jnp.cos(angle), jnp.sin(angle)

    fine = 16
    ca, sa, cb, sb = lax.optimization_barrier(pair(quarter // fine, fine) + pair(fine, 1))
    ca, sa, cb, sb = ca[:, :, None], sa[:, :, None], cb[:, None], sb[:, None]
    cos_part = ((ca * cb - sa * sb) * factor).reshape(2, quarter, half)
    sin_part = ((sa * cb + ca * sb) * factor).reshape(2, quarter, half)
    row = lax.broadcasted_iota(jnp.int32, sin_part.shape, 1)
    column = lax.broadcasted_iota(jnp.int32, sin_part.shape, 2)
    alternate = (1 - 2 * (column % 2)).astype(jnp.float32) * factor
    sin_part = jnp.where(row == 0, alternate, sin_part)
    return jnp.concatenate(
        [cos_part.astype(jnp.bfloat16), sin_part.astype(jnp.bfloat16)], axis=1
    )


def round16(value):
    return value.astype(jnp.bfloat16).astype(jnp.float32)


def unpack(index_ref, keys):
    depth = index_ref.shape[1]

    def block(g, carry):
        word = index_ref[g]
        mu = word // 65536
        key = (word - mu * 65536) * MUBINS + mu
        upper = key // LOW
        rows = pl.ds(pl.multiple_of(g * depth, depth), depth)
        keys[0, rows, :] = (key - upper * LOW).astype(jnp.float32)
        keys[1, rows, :] = upper.astype(jnp.float32)
        return carry

    lax.fori_loop(0, index_ref.shape[0], block, 0)


def products(table_ref, lines_ref, prod, parity):
    half = table_ref.shape[1]

    def group(f, carry):
        right = lines_ref[f, :, parity].reshape(half, lines_ref.shape[-1])

        def rows_of(i, inner):
            rows = pl.ds(pl.multiple_of(i * 256, 256), 256)
            prod[f, parity, rows, :] = jnp.dot(
                table_ref[parity, rows, :], right, preferred_element_type=jnp.float32
            )
            return inner

        return lax.fori_loop(0, half // 256, rows_of, carry)

    lax.fori_loop(0, prod.shape[0], group, 0)


def local_kernel(length, table_ref, lines_ref, index_ref, wave_ref, out_ref, prod, vals, keys):
    unpack(index_ref, keys)
    products(table_ref, lines_ref, prod, 0)
    products(table_ref, lines_ref, prod, 1)
    bins(length, wave_ref, out_ref, prod, vals, keys)


def exchange_kernel(
    length, field_count, gz_count, table_ref, lines_ref, index_ref, wave_ref, out_ref,
    prod, vals, keys, lines, index, send, recv, own, index_send, index_recv, index_own,
):
    devices = field_count * gz_count
    me_field, me_gz = lax.axis_index("field"), lax.axis_index("gz")
    far = gz_count // 2
    mine = (gz_count - far) * field_count

    def peer(step):
        f = lax.rem(me_field + lax.rem(step, field_count), field_count)
        g = lax.rem(me_gz + step // field_count + far, gz_count)
        return f, g

    def others(run):
        def loop(step, carry):
            run(step)
            return carry

        lax.fori_loop(0, mine, loop, 0)
        lax.fori_loop(mine + 1, devices, loop, 0)

    def along(run):
        def loop(step, carry):
            run(step)
            return carry

        lax.fori_loop(1, gz_count, loop, 0)

    barrier = pltpu.get_barrier_semaphore()
    others(
        lambda step: pl.semaphore_signal(
            barrier, inc=1, device_id=peer(step), device_id_type=pl.DeviceIdType.MESH
        )
    )
    pl.semaphore_wait(barrier, devices - 1)

    def index_copy(step):
        g = lax.rem(me_gz + step, gz_count)
        return pltpu.make_async_remote_copy(
            src_ref=index_ref.at[g],
            dst_ref=index.at[me_gz],
            send_sem=index_send.at[step],
            recv_sem=index_recv.at[step],
            device_id=(me_field, g),
            device_id_type=pl.DeviceIdType.MESH,
        )

    def lines_copy(parity):
        def copy(step):
            f, g = peer(step)
            return pltpu.make_async_remote_copy(
                src_ref=lines_ref.at[f * gz_count + g, parity],
                dst_ref=lines.at[me_field, me_gz, parity],
                send_sem=send.at[parity, step],
                recv_sem=recv.at[parity, step],
                device_id=(f, g),
                device_id_type=pl.DeviceIdType.MESH,
            )

        return copy

    along(lambda step: index_copy(step).start())
    for parity in range(2):
        others(lambda step: lines_copy(parity)(step).start())
    me = me_field * gz_count + me_gz
    kept = [
        pltpu.make_async_copy(
            lines_ref.at[me, parity], lines.at[me_field, me_gz, parity], own.at[parity]
        )
        for parity in range(2)
    ]
    kept_index = pltpu.make_async_copy(index_ref.at[me_gz], index.at[me_gz], index_own)
    for copy in kept + [kept_index]:
        copy.start()

    kept_index.wait()
    along(lambda step: index_copy(step).wait_recv())
    unpack(index, keys)
    for parity in range(2):
        kept[parity].wait()
        others(lambda step: lines_copy(parity)(step).wait_recv())
        products(table_ref, lines, prod, parity)
    bins(length, wave_ref, out_ref, prod, vals, keys)
    along(lambda step: index_copy(step).wait_send())
    for parity in range(2):
        others(lambda step: lines_copy(parity)(step).wait_send())


def bins(length, wave_ref, out_ref, prod, vals, keys):
    quarter, half = length // 4, length // 2
    groups, local = prod.shape[0], prod.shape[3] // (2 * LANES)
    fields = groups * local
    out_ref[...] = jnp.zeros_like(out_ref)
    wave_x = wave_ref[0:1, :]
    wave_y = wave_ref[1:2, :]
    low_iota = lax.broadcasted_iota(jnp.int32, (16, LANES), 0).astype(jnp.float32)
    iotas = [(low_iota + 16.0 * j).astype(jnp.bfloat16) for j in range(LANES // 16)]
    one = jnp.ones((16, LANES), jnp.bfloat16)
    none = jnp.zeros((16, LANES), jnp.bfloat16)

    def cell_row(j, k):
        start = 1 - (k + quarter - 1) // quarter
        return (
            k,
            half - k,
            half + k - quarter * start,
            length - k - quarter * start,
        )[j]

    def tile(t, carry):
        first = pl.multiple_of(t * 8, 8)
        row = lax.broadcasted_iota(jnp.int32, (8, LANES), 0) + first
        special = row == 0

        def load(a, c, parity, sine):
            g, i = a // local, a % local
            at = (c * local + i) * LANES
            return prod[g, parity, pl.ds(sine * quarter + first, 8), at : at + LANES]

        def spectra(a):
            parts = []
            for c in range(2):
                ec, oc = load(a, c, 0, 0), load(a, c, 1, 0)
                es, os = load(a, c, 0, 1), load(a, c, 1, 1)
                p, q, m, n = ec + oc, es + os, ec - oc, os - es
                parts.append(
                    (
                        (p, jnp.where(special, 0.0, q)),
                        (m, jnp.where(special, 0.0, n)),
                        (jnp.where(special, es, m), jnp.where(special, os, -n)),
                        (jnp.where(special, es, p), jnp.where(special, -os, -q)),
                    )
                )
            u, v = parts
            return [(u[j][0] + v[j][1], v[j][0] - u[j][1]) for j in range(4)]

        k = row.astype(jnp.float32)
        zero_wave = (0.0, -half, quarter, -quarter)
        waves = (k, half - k, k - half, -k)
        base = spectra(0)
        second = None
        totals = [None] * 4
        saved = [None] * 4
        pending = [None] * 4
        for a in range(fields):
            spec = base if a == 0 else spectra(a)
            for j in range(4):
                cross = base[j][0] * spec[j][0] + base[j][1] * spec[j][1]
                if a == 0:
                    wz = jnp.where(special, float(zero_wave[j]), waves[j])
                    square = wave_x * wave_x + wave_y * wave_y + wz * wz
                    saved[j] = (wz, 1.0 / square)
                    vals[0, j * 8 : j * 8 + 8] = round16(cross)
                    continue
                wz, inverse = saved[j]
                if a == 1:
                    vals[1, j * 8 : j * 8 + 8] = round16(cross)
                    term = -0.5 * cross
                else:
                    weight = (
                        1.5 * wave_x * wave_x,
                        1.5 * wave_y * wave_y,
                        1.5 * wz * wz,
                        3.0 * wave_x * wave_y,
                        3.0 * wave_x * wz,
                        3.0 * wave_y * wz,
                    )[a - 2]
                    term = weight * inverse * cross
                pending[j] = term if pending[j] is None else pending[j] + term
                if a % local == local - 1:
                    rounded = round16(pending[j])
                    totals[j] = rounded if totals[j] is None else totals[j] + rounded
                    pending[j] = None
        for j in range(4):
            high = round16(totals[j])
            vals[2, j * 8 : j * 8 + 8] = high
            vals[3, j * 8 : j * 8 + 8] = totals[j] - high
        total = out_ref[...]
        for start in range(0, 32, PAIRS):
            left, hot = [], []
            for r in range(start, start + PAIRS):
                cell = cell_row(r // 8, first + r % 8)
                spread = [
                    jnp.broadcast_to(part, (16, LANES)).astype(jnp.bfloat16)
                    for part in [vals[i, r : r + 1] for i in range(4)]
                    + [keys[i, pl.ds(cell, 1), :] for i in range(2)]
                ]
                match = spread[4] == iotas[0]
                left.append(
                    jnp.concatenate(
                        [jnp.where(match, spread[i], none) for i in range(4)]
                        + [jnp.where(match, one, none)],
                        axis=0,
                    )
                )
                hot.append(
                    jnp.concatenate(
                        [jnp.where(spread[5] == it, one, none) for it in iotas], axis=0
                    )
                )
            total = total + lax.dot_general(
                jnp.concatenate(left, axis=1),
                jnp.concatenate(hot, axis=1),
                (((1,), (1,)), ((), ())),
                preferred_element_type=jnp.float32,
            )
        out_ref[...] = total
        return carry

    lax.fori_loop(0, quarter // 8, tile, 0)


def relayout_kernel(fields_ref, out_ref):
    for c in range(2):
        for i in range(fields_ref.shape[2]):
            at = (c * fields_ref.shape[2] + i) * LANES
            for h in range(out_ref.shape[1]):
                block = fields_ref[:, c, i, :, h * LANES : (h + 1) * LANES]
                block = block.reshape(16, 2, block.shape[1], LANES)
                for parity in range(2):
                    out_ref[:, h, parity, :, at : at + LANES] = jnp.swapaxes(
                        block[:, parity], 0, 1
                    )


def relayout(fields):
    depth, _, local, planes, yrows = fields.shape
    parts = yrows // LANES
    out = pl.pallas_call(
        relayout_kernel,
        grid=(depth // 32,),
        out_shape=jax.ShapeDtypeStruct(
            (planes, parts, 2, depth // 2, 2 * local * LANES), fields.dtype
        ),
        in_specs=[pl.BlockSpec((32, 2, local, planes, yrows), lambda i: (i, 0, 0, 0, 0))],
        out_specs=pl.BlockSpec(
            (planes, parts, 2, 16, 2 * local * LANES), lambda i: (0, 0, 0, i, 0)
        ),
    )(fields)
    return out.reshape(planes * parts, 2, depth // 2, 2 * local * LANES)


def reduce_kernel(field_count, gz_count, mine_ref, out_ref, parts, answer, send, recv, send2, recv2):
    devices = field_count * gz_count
    me_field, me_gz = lax.axis_index("field"), lax.axis_index("gz")
    me = me_field * gz_count + me_gz

    def peer(step):
        other = lax.rem(me + step, devices)
        return other, (other // gz_count, lax.rem(other, gz_count))

    barrier = pltpu.get_barrier_semaphore()

    def greet(step, carry):
        _, place = peer(step)
        pl.semaphore_signal(
            barrier, inc=1, device_id=place, device_id_type=pl.DeviceIdType.MESH
        )
        return carry

    lax.fori_loop(1, devices, greet, 0)
    pl.semaphore_wait(barrier, devices - 1)

    def scatter(step):
        other, place = peer(step)
        return pltpu.make_async_remote_copy(
            src_ref=mine_ref.at[other],
            dst_ref=parts.at[step],
            send_sem=send.at[step],
            recv_sem=recv.at[step],
            device_id=place,
            device_id_type=pl.DeviceIdType.MESH,
        )

    def gather(step):
        _, place = peer(step)
        return pltpu.make_async_remote_copy(
            src_ref=answer,
            dst_ref=out_ref.at[me],
            send_sem=send2.at[step],
            recv_sem=recv2.at[step],
            device_id=place,
            device_id_type=pl.DeviceIdType.MESH,
        )

    def start(copy):
        def run(step, carry):
            copy(step).start()
            return carry

        lax.fori_loop(1, devices, run, 0)

    start(scatter)

    def collect(step, total):
        scatter(step).wait_recv()
        return total + parts[step]

    answer[...] = lax.fori_loop(1, devices, collect, mine_ref[me])
    start(gather)
    out_ref[me] = answer[...]

    def finish(step, carry):
        scatter(step).wait_send()
        gather(step).wait()
        return carry

    lax.fori_loop(1, devices, finish, 0)


def all_reduce(total, field_count, gz_count):
    devices = field_count * gz_count
    rows = max(1, total.shape[0] // devices)
    total = jnp.pad(total, ((0, devices * rows - total.shape[0]), (0, 0)))
    total = total.reshape(devices, rows, LANES)
    return pl.pallas_call(
        functools.partial(reduce_kernel, field_count, gz_count),
        out_shape=jax.ShapeDtypeStruct(total.shape, jnp.float32),
        in_specs=[pl.BlockSpec(memory_space=pltpu.VMEM)],
        out_specs=pl.BlockSpec(memory_space=pltpu.VMEM),
        scratch_shapes=[
            pltpu.VMEM(total.shape, jnp.float32),
            pltpu.VMEM(total.shape[1:], jnp.float32),
            pltpu.SemaphoreType.DMA((devices,)),
            pltpu.SemaphoreType.DMA((devices,)),
            pltpu.SemaphoreType.DMA((devices,)),
            pltpu.SemaphoreType.DMA((devices,)),
        ],
        compiler_params=pltpu.CompilerParams(collective_id=0, has_side_effects=True),
    )(total).reshape(devices * rows, LANES)


def body(fields, shells, mubins):
    depth_local, _, local_fields, planes, yrows = fields.shape
    gz_count, field_count = lax.axis_size("gz"), lax.axis_size("field")
    devices = gz_count * field_count
    length = depth_local * gz_count
    half = length // 2
    plane_rows = planes * yrows
    width = plane_rows // devices
    me_gz, me_field = lax.axis_index("gz"), lax.axis_index("field")

    exchange = width == LANES and depth_local % 32 == 0
    if exchange:
        lines = relayout(fields)
    else:
        lines = fields.reshape(depth_local // 2, 2, 2, local_fields, devices, width)
        lines = lines.transpose(4, 1, 0, 2, 3, 5).reshape(
            devices, 2, depth_local // 2, 2 * local_fields * width
        )

    share = planes // field_count
    shells, mubins = (
        lax.dynamic_slice_in_dim(ids, me_field * share, share, 1) for ids in (shells, mubins)
    )
    index = (shells + mubins * 65536).reshape(depth_local, gz_count, width).transpose(1, 0, 2)

    span = 2 * local_fields * LANES
    table = quarter_tables(length, jnp.minimum(me_gz, 0))
    column = (me_field * gz_count + me_gz) * width + jnp.arange(LANES, dtype=jnp.int32)
    waves = jnp.stack([length // 4 + column // yrows, length // 8 + column % yrows])
    waves = jnp.pad(waves.astype(jnp.float32), ((0, 6), (0, 0)))
    landed = (field_count, gz_count, 2, depth_local // 2, span)
    scratch = [
        pltpu.VMEM((field_count, 2, half, span), jnp.float32),
        pltpu.VMEM((4, 32, LANES), jnp.float32),
        pltpu.VMEM((2, length, LANES), jnp.float32),
    ]
    vmem, anywhere = pl.BlockSpec(memory_space=pltpu.VMEM), pl.BlockSpec(memory_space=pl.ANY)
    if exchange:
        run, places, wide = (
            functools.partial(exchange_kernel, length, field_count, gz_count),
            anywhere,
            dict(collective_id=1, has_side_effects=True),
        )
        scratch += [
            pltpu.VMEM(landed, jnp.bfloat16),
            pltpu.VMEM((gz_count, depth_local, LANES), jnp.int32),
            pltpu.SemaphoreType.DMA((2, devices)),
            pltpu.SemaphoreType.DMA((2, devices)),
            pltpu.SemaphoreType.DMA((2,)),
            pltpu.SemaphoreType.DMA((gz_count,)),
            pltpu.SemaphoreType.DMA((gz_count,)),
            pltpu.SemaphoreType.DMA,
        ]
    else:
        run, places, wide = functools.partial(local_kernel, length), vmem, {}
        lines = lax.all_to_all(lines, ("field", "gz"), split_axis=0, concat_axis=0, tiled=True)
        lines = lines.reshape(landed[:-1] + (2 * local_fields, width))
        lines = jnp.pad(lines, ((0, 0),) * 5 + ((0, LANES - width),)).reshape(landed)
        index = lax.all_to_all(index, "gz", split_axis=0, concat_axis=0, tiled=True)
        index = jnp.pad(index, ((0, 0), (0, 0), (0, LANES - width)), constant_values=SHELLS)

    total = pl.pallas_call(
        run,
        out_shape=jax.ShapeDtypeStruct((ROWS * LOW, LANES), jnp.float32),
        in_specs=[vmem, places, places, vmem],
        out_specs=vmem,
        scratch_shapes=scratch,
        compiler_params=pltpu.CompilerParams(vmem_limit_bytes=56 * 1024 * 1024, **wide),
    )(table, lines, index, waves)

    total = total.reshape(ROWS, LOW, LANES)
    total = jnp.concatenate([total[:2], total[2:3] + total[3:4], total[4:]])
    total = all_reduce(total.reshape(-1, LANES), field_count, gz_count)[: 4 * LOW]
    total = total.reshape(4, 2, MUBINS, LANES).transpose(0, 2, 3, 1)
    total = total.reshape(4, MUBINS, SHELLS)
    return total[:3] / jnp.maximum(total[3], 1.0)[None]


def solution(mesh):
    in_specs = (P("gz", None, "field", None, None), P("gz", None, None), P("gz", None, None))
    return jax.shard_map(body, mesh=mesh, in_specs=in_specs, out_specs=P(), check_vma=False)
```
